32 devices in a mesh: va: 4 (over z), vb: 2 (over core), occ: 4 (over y, x).
Axes of the slice: x: 2, y: 2, z: 4, core: 2. Of those that a mesh axis runs over, the one named last changes fastest.
Arguments:
- amplitudes: bfloat16 [6, 1536, 1536], P(None, 'va', 'occ'), may hold values from -6 to 6
- bra_factor: bfloat16 [4, 1536, 1536], P('vb', 'va'), may hold values from -0.15625 to 0.15625
- ket_factor: bfloat16 [4, 1536, 1536], P('va', ('vb', 'occ')), may hold values from -0.15625 to 0.15625
- pair_list: int32 [2, 4], replicated, may hold values from 0 to 5, as said below
Outputs:
- ladder: float32 [6, 1536, 1536], P(None, 'va', ('vb', 'occ'))
The draws below stay inside these ranges and needn't reach their ends.
Inputs may be any that keep to these rules, and one draw needn't show every extreme that they name: `pair_list`: each row names 4 different pairs, and every pair of 0 to 5 is named by some row.
All inputs are finite; a program needn't handle non-finite values.
Results may differ from the reference program's by a relative error of at most 0.0042.
Values may be sent and summed in bfloat16 or wider, within the bound.
A program may use at most 64 MiB of HBM per device.

```python
import jax
import jax.numpy as jnp

NV = 1536
QC = 1
SPANS = 2
PAIRS = 6
PICK = 4
NQW = 4
N_VB = 2


def draw_pair_list(key, part):
    order = jax.random.permutation(jax.random.fold_in(key, 17), PAIRS)
    places = (jnp.arange(N_VB, dtype=jnp.int32)[:, None] * PICK + jnp.arange(PICK, dtype=jnp.int32)[None, :]) % PAIRS
    return order[places].astype(jnp.int32)


def spiked(array, key, source, target, parts, factor):
    def block_of(position):
        return (jnp.arange(array.shape[position]) // (array.shape[position] // parts)).reshape((-1,) + (1,) * (array.ndim - 1 - position))

    first = jax.random.permutation(key, parts)[block_of(target)]
    second = (block_of(target) + parts // 2) % parts
    return jnp.where((block_of(source) == first) | (block_of(source) == second), factor * array, array)


def level_of(own_key, dims, cuts, low, largest):
    factor_of, own = 1.0, jax.random.fold_in(own_key, 6)
    for dim, parts in cuts:
        draws = jnp.exp(jax.random.uniform(jax.random.fold_in(own, dim), (parts,), jnp.float32, low / len(cuts), largest / len(cuts)))
        factor_of = factor_of * jnp.repeat(draws, dims[dim] // parts).reshape([-1 if axis == dim else 1 for axis in range(len(dims))])
    return factor_of


def normal_values(own_key, shape, scale, most, split=(), kind=jnp.bfloat16):
    factor_of = level_of(own_key, shape, split, -0.22, 0.18) if split else 1.0
    drawn = jax.random.normal(own_key, shape, jnp.float32) * scale * factor_of
    return jnp.minimum(jnp.maximum(drawn, -most), most).astype(kind)


def gaussian_with(rng, shape, scale, reach, shards, heavy, kind=jnp.bfloat16):
    entries = scale * jax.random.normal(rng, shape, jnp.float32)
    if shards:
        entries = entries * level_of(rng, shape, shards, -0.22, 0.18)
    return jnp.clip(spiked(entries, jax.random.fold_in(rng, 3), *heavy), -reach, reach).astype(kind)


def setup_inputs(seed: int = 0) -> dict:
    key_list = jax.random.split(jax.random.key(seed), 5)
    return {
        "amplitudes": normal_values(key_list[0], (PAIRS, NV, NV), 1.0, 6.0, ((1, 4), (2, 4))),
        "bra_factor": gaussian_with(key_list[1], (NQW, NV, NV), (NV * QC * SPANS * N_VB // 2) ** -0.5, 0.15625, ((0, 2), (1, 4)), (1, 2, 4, 2.0)),
        "ket_factor": normal_values(key_list[2], (NQW, NV, NV), NV ** -0.5, 0.15625, ((0, 4), (1, 8))),
        "pair_list": draw_pair_list(jax.random.fold_in(key_list[4], 71), 0),
    }


def reference(amplitudes, bra_factor, ket_factor, pair_list):
    group = QC * SPANS
    ladder = jnp.zeros((PAIRS, NV, NV), jnp.float32)
    for step in range(N_VB):
        picks = pair_list[step]
        ket_group = ket_factor[step * group:(step + 1) * group].astype(jnp.float32)
        bra_group = bra_factor[step * group:(step + 1) * group].astype(jnp.float32)
        chosen = jnp.take(amplitudes, picks, axis=0).astype(jnp.float32)
        half = jnp.einsum('qbd,kcd->qkcb', ket_group, chosen).astype(jnp.bfloat16)
        partial_terms = jnp.einsum('qca,qkcb->kab', bra_group, half.astype(jnp.float32))
        ladder = ladder.at[picks].add(partial_terms)
    return ladder
```

```python
import functools

import jax
import jax.numpy as jnp
from jax import lax
from jax.experimental import pallas as pl
from jax.experimental.pallas import tpu as pltpu
from jax.sharding import PartitionSpec as P

MESH = pl.DeviceIdType.MESH
NT = (((1,), (1,)), ((), ()))


def from_behind(block, axis, distance):
    devices = range(lax.axis_size(axis))
    route = [((i - distance) % len(devices), i) for i in devices]
    return lax.ppermute(block, axis, route)


def per_device(amplitudes, bra_factor, ket_factor, pair_list):
    tau_rows = lax.all_gather(amplitudes, "occ", axis=2, tiled=True)
    ket_rows = lax.all_gather(ket_factor, "va", axis=0, tiled=True)
    group = bra_factor.shape[0]
    pairs = amplitudes.shape[0]
    cycle_size = lax.axis_size("vb")
    position = lax.axis_index("vb")
    total = jnp.zeros((pairs, bra_factor.shape[2], ket_factor.shape[1]), jnp.float32)
    travelling = bra_factor
    for step in range(cycle_size):
        if step > 0:
            travelling = from_behind(travelling, "vb", 1)
        which = (position - step) % cycle_size
        picks = lax.dynamic_index_in_dim(pair_list, which, 0, keepdims=False)
        chosen = jnp.take(tau_rows, picks, axis=0)
        ket_group = lax.dynamic_slice_in_dim(ket_rows, which * group, group, 0)
        half = jnp.einsum(
            "qbd,kcd->qkcb", ket_group, chosen, preferred_element_type=jnp.float32
        ).astype(jnp.bfloat16)
        partial_terms = jnp.einsum(
            "qca,qkcb->kab", travelling, half, preferred_element_type=jnp.float32
        )
        total = total.at[picks].add(partial_terms)
    return lax.psum_scatter(total, "va", scatter_dimension=1, tiled=True)


def ladder_kernel(
    n, chunks, list_ref, tau_in, bra_in, ket_in, out_ref,
    tau, bra, ket, half, part, outgoing, from_left, from_right,
    local_sem, own_send, own_recv, relay_send, relay_recv, pass_send, pass_recv,
    bra_send, bra_recv, kr_send, kl_recv, kl_send, kr_recv,
    sum_send, left_recv, right_recv,
):
    z, v, o = lax.axis_index("va"), lax.axis_index("vb"), lax.axis_index("occ")
    pairs, c_rows, width = tau_in.shape
    spins = pairs // chunks
    b_rows = ket_in.shape[1]
    part_b = b_rows // chunks
    groups, picks = list_ref.shape
    group = bra_in.shape[0]
    pieces = chunks * spins
    batch = pairs // spins
    xo = o + 1 - 2 * lax.rem(o, 2)
    yo = lax.rem(o + 2, 4)
    do = 3 - o
    sibling = (z, 1 - v, o)
    x_near, y_near = (z, v, xo), (z, v, yo)
    right, left = (z + 1, v, o), (z - 1, v, o)
    has_right, has_left = z < n - 1, z > 0

    def remote(src, dst, send, recv, device):
        return pltpu.make_async_remote_copy(
            src_ref=src, dst_ref=dst, send_sem=send, recv_sem=recv,
            device_id=device, device_id_type=MESH,
        )

    locals_ = [
        pltpu.make_async_copy(tau_in, tau.at[o], local_sem.at[0]),
        pltpu.make_async_copy(ket_in, ket.at[pl.ds(z, 1)], local_sem.at[1]),
        pltpu.make_async_copy(bra_in, bra.at[v], local_sem.at[2]),
    ]
    for copy in locals_:
        copy.start()

    barrier = pltpu.get_barrier_semaphore()
    for near in (sibling, x_near, y_near):
        pl.semaphore_signal(barrier, inc=1, device_id=near, device_id_type=MESH)

    @pl.when(has_right)
    def _():
        pl.semaphore_signal(barrier, inc=1, device_id=right, device_id_type=MESH)

    @pl.when(has_left)
    def _():
        pl.semaphore_signal(barrier, inc=1, device_id=left, device_id_type=MESH)

    pl.semaphore_wait(
        barrier, 3 + jnp.where(has_right, 1, 0) + jnp.where(has_left, 1, 0)
    )

    rows = c_rows // 2
    mine = pl.ds(pl.multiple_of(v * rows, rows), rows)
    other = pl.ds(pl.multiple_of((1 - v) * rows, rows), rows)

    def own(p, way):
        return remote(
            tau_in.at[p, mine], tau.at[o, p, mine],
            own_send.at[way, p], own_recv.at[way, p], (x_near, y_near)[way],
        )

    def own_arrival(p, way):
        block = tau.at[(xo, yo)[way], p, mine]
        return remote(block, block, own_send.at[way, p], own_recv.at[way, p], (x_near, y_near)[way])

    relay_from = jnp.where(v == 0, xo, yo)
    relay_to = (z, v, jnp.where(v == 0, yo, xo))

    def relay(p):
        block = tau.at[relay_from, p, mine]
        return remote(block, block, relay_send.at[p], relay_recv.at[p], relay_to)

    def relay_arrival(p):
        block = tau.at[do, p, mine]
        return remote(block, block, relay_send.at[p], relay_recv.at[p], relay_to)

    def handed(p, k, which):
        block = tau.at[(xo, yo, do)[k], p, which]
        return remote(block, block, pass_send.at[k, p], pass_recv.at[k, p], sibling)

    ahead = 3

    def comm(p):
        own_arrival(p, 0).wait_recv()
        own_arrival(p, 1).wait_recv()
        relay(p).start()
        handed(p, 0, mine).start()
        handed(p, 1, mine).start()
        if p + ahead < pairs:
            own(p + ahead, 0).start()
            own(p + ahead, 1).start()

    def comm_far(p):
        relay_arrival(p).wait_recv()
        handed(p, 2, mine).start()

    def chunk(q, h):
        return ket.at[q, pl.ds(h * part_b, part_b)]

    def to_right(h, hop):
        if hop == 0:
            src = ket_in.at[0, pl.ds(h * part_b, part_b)]
        else:
            src = chunk(z - hop, h)
        return remote(src, chunk(z - hop, h), kr_send.at[hop, h], kl_recv.at[hop, h], right)

    def to_left(h, hop):
        if hop == 0:
            src = ket_in.at[0, pl.ds(h * part_b, part_b)]
        else:
            src = chunk(z + hop, h)
        return remote(src, chunk(z + hop, h), kl_send.at[hop, h], kr_recv.at[hop, h], left)

    def comm_ket(h, hop):
        if hop > 0:
            @pl.when(z - hop >= 0)
            def _():
                block = chunk(z - hop, h)
                remote(block, block, kr_send.at[hop - 1, h], kl_recv.at[hop - 1, h], left).wait_recv()

            @pl.when(z + hop <= n - 1)
            def _():
                block = chunk(z + hop, h)
                remote(block, block, kl_send.at[hop - 1, h], kr_recv.at[hop - 1, h], right).wait_recv()
        if hop < n - 1:
            @pl.when((z - hop >= 0) & has_right)
            def _():
                to_right(h, hop).start()

            @pl.when((z + hop <= n - 1) & has_left)
            def _():
                to_left(h, hop).start()

    def weight(g, p):
        total = jnp.float32(0.0)
        for k in range(picks):
            total = total + jnp.where(list_ref[g, k] == p, 1.0, 0.0)
        return total

    def sum_right(i, t):
        return remote(outgoing.at[i, t], from_left.at[i, t], sum_send.at[i, t], left_recv.at[i, t], right)

    def sum_left(i, t):
        return remote(outgoing.at[i, t], from_right.at[i, t], sum_send.at[i, t], right_recv.at[i, t], left)

    def left_arrival(i, t):
        block = from_left.at[i, t]
        return remote(block, block, sum_send.at[i, t], left_recv.at[i, t], left)

    def right_arrival(i, t):
        block = from_right.at[i, t]
        return remote(block, block, sum_send.at[i, t], right_recv.at[i, t], right)

    order = []
    for k in range((n + 1) // 2):
        order += [n - 1 - k] + ([k] if k != n - 1 - k else [])
    a_rows = bra.shape[3] // n

    def compute(i):
        h, turn = i // spins, lax.rem(i, spins)
        rows_h = pl.ds(pl.multiple_of(h * part_b, part_b), part_b)
        for s in range(batch):
            p = turn * batch + s
            total = None
            for j in range(4):
                lhs = ket[:, rows_h, pl.ds(j * width, width)].reshape(n * part_b, width)
                term = lax.dot_general(lhs, tau[j, p], NT, preferred_element_type=jnp.float32)
                total = term if total is None else total + term
            for q in range(n):
                block = total[q * part_b:(q + 1) * part_b] * weight(q // group, p)
                half[pl.ds(s * part_b, part_b), pl.ds(q * c_rows, c_rows)] = block.astype(jnp.bfloat16)
        for t in order:
            cols = pl.ds(t * a_rows, a_rows)
            right_side = bra[:, :, :, cols].reshape(n * c_rows, a_rows)
            block = jnp.dot(half[...], right_side, preferred_element_type=jnp.float32)
            part[i, t] = block
            if t > 0:
                @pl.when(z == 0)
                def _():
                    outgoing[i, t] = block.astype(jnp.bfloat16)
                    sum_right(i, t).start()
            if t < n - 1:
                @pl.when(z == n - 1)
                def _():
                    outgoing[i, t] = block.astype(jnp.bfloat16)
                    sum_left(i, t).start()

    def combine(i):
        for t in order:
            if t > 1:
                @pl.when((z > 0) & (z < t))
                def _():
                    left_arrival(i, t).wait_recv()
                    outgoing[i, t] = (part[i, t] + from_left[i, t].astype(jnp.float32)).astype(jnp.bfloat16)
                    sum_right(i, t).start()
            if t < n - 2:
                @pl.when((z < n - 1) & (z > t))
                def _():
                    right_arrival(i, t).wait_recv()
                    outgoing[i, t] = (part[i, t] + from_right[i, t].astype(jnp.float32)).astype(jnp.bfloat16)
                    sum_left(i, t).start()

    def finish(i):
        for t in range(n):
            @pl.when(z == t)
            def _():
                if t > 0:
                    left_arrival(i, t).wait_recv()
                    part[i, t] += from_left[i, t].astype(jnp.float32)
                if t < n - 1:
                    right_arrival(i, t).wait_recv()
                    part[i, t] += from_right[i, t].astype(jnp.float32)

    bra_copy = remote(bra_in, bra.at[v], bra_send, bra_recv, sibling)
    for p in range(min(ahead, pairs)):
        own(p, 0).start()
        own(p, 1).start()
    comm_ket(0, 0)
    bra_copy.start()
    for copy in locals_:
        copy.wait()

    def gather(h, first):
        for s in range(max(batch, n)):
            p = first * batch + s
            if first < spins and s < batch:
                comm(p)
                if s > 0:
                    comm_far(p - 1)
            if s + 1 < n:
                comm_ket(h, s + 1)
            if s == 0 and h + 1 < chunks:
                comm_ket(h + 1, 0)
        if first < spins:
            comm_far(first * batch + batch - 1)
            for s in range(batch):
                for k in range(3):
                    handed(first * batch + s, k, other).wait_recv()

    gather(0, 0)
    remote(bra_in, bra.at[1 - v], bra_send, bra_recv, sibling).wait_recv()
    compute(0)
    for step in range(1, max(chunks, spins)):
        gather(step, step) if step < chunks else None
        if step == 1:
            compute(1)
            combine(0)

    def turn(i, carry):
        compute(i)
        combine(i - 1)
        return carry

    lax.fori_loop(2, pieces, turn, 0)
    combine(pieces - 1)

    def close(i, carry):
        finish(i)
        return carry

    lax.fori_loop(0, pieces, close, 0)
    for p in range(pairs):
        slot, s = p // batch, p % batch
        full = jnp.concatenate(
            [part[h * spins + slot, z, pl.ds(s * part_b, part_b), :] for h in range(chunks)], axis=0
        )
        out_ref[p] = full.T

    for p in range(pairs):
        own(p, 0).wait_send()
        own(p, 1).wait_send()
        relay(p).wait_send()
        for k in range(3):
            handed(p, k, mine).wait_send()
    bra_copy.wait_send()
    for h in range(chunks):
        for hop in range(n - 1):
            @pl.when((z - hop >= 0) & has_right)
            def _():
                to_right(h, hop).wait_send()

            @pl.when((z + hop <= n - 1) & has_left)
            def _():
                to_left(h, hop).wait_send()

    def drain(i, carry):
        for t in range(n):
            @pl.when(z < t)
            def _():
                sum_right(i, t).wait_send()

            @pl.when(z > t)
            def _():
                sum_left(i, t).wait_send()
        return carry

    lax.fori_loop(0, pieces, drain, 0)


def fused_device(n, chunks, amplitudes, bra_factor, ket_factor, pair_list):
    pairs, c_rows, width = amplitudes.shape
    b_rows, depth = ket_factor.shape[1:]
    group, _, columns = bra_factor.shape
    pieces = pairs
    tall = pairs // (pairs // chunks) * (b_rows // chunks)
    a_rows = columns // n
    dma = pltpu.SemaphoreType.DMA
    hbm = pl.BlockSpec(memory_space=pl.ANY)
    return pl.pallas_call(
        functools.partial(ladder_kernel, n, chunks),
        out_shape=jax.ShapeDtypeStruct((pairs, a_rows, b_rows), jnp.float32),
        in_specs=[pl.BlockSpec(memory_space=pltpu.SMEM), hbm, hbm, hbm],
        out_specs=pl.BlockSpec(memory_space=pltpu.VMEM),
        scratch_shapes=[
            pltpu.VMEM((4, pairs, c_rows, width), jnp.bfloat16),
            pltpu.VMEM((2, group, c_rows, columns), jnp.bfloat16),
            pltpu.VMEM((n, b_rows, depth), jnp.bfloat16),
            pltpu.VMEM((tall, n * c_rows), jnp.bfloat16),
            pltpu.VMEM((pieces, n, tall, a_rows), jnp.float32),
            pltpu.VMEM((pieces, n, tall, a_rows), jnp.bfloat16),
            pltpu.VMEM((pieces, n, tall, a_rows), jnp.bfloat16),
            pltpu.VMEM((pieces, n, tall, a_rows), jnp.bfloat16),
            dma((3,)),
            dma((2, pairs)), dma((2, pairs)),
            dma((pairs,)), dma((pairs,)),
            dma((3, pairs)), dma((3, pairs)),
            dma, dma,
            dma((n, chunks)), dma((n, chunks)), dma((n, chunks)), dma((n, chunks)),
            dma((pieces, n)), dma((pieces, n)), dma((pieces, n)),
        ],
        compiler_params=pltpu.CompilerParams(
            collective_id=0, has_side_effects=True, vmem_limit_bytes=60 * 2**20
        ),
    )(pair_list, amplitudes, bra_factor, ket_factor)


def solution(mesh):
    placed = (P(None, "va", "occ"), P("vb", "va", None), P("va", ("vb", "occ"), None), P())
    n = mesh.shape["va"]
    small = mesh.shape["vb"] == 2 and mesh.shape["occ"] == 4

    def body(amplitudes, bra_factor, ket_factor, pair_list):
        chunks = 3
        fits = (
            small
            and amplitudes.shape[0] == 2 * chunks
            and ket_factor.shape[0] == 1
            and 2 * bra_factor.shape[0] == n
            and ket_factor.shape[1] % (16 * chunks) == 0
        )
        if fits:
            return fused_device(n, chunks, amplitudes, bra_factor, ket_factor, pair_list)
        return per_device(amplitudes, bra_factor, ket_factor, pair_list)

    return jax.shard_map(
        body,
        mesh=mesh,
        in_specs=placed,
        out_specs=P(None, "va", ("vb", "occ")),
        check_vma=False,
    )
```

```python
import functools

import jax
import jax.numpy as jnp
from jax import lax
from jax.experimental import pallas as pl
from jax.experimental.pallas import tpu as pltpu
from jax.sharding import PartitionSpec as P

MESH = pl.DeviceIdType.MESH
NT = (((1,), (1,)), ((), ()))


def from_behind(block, axis, distance):
    devices = range(lax.axis_size(axis))
    route = [((i - distance) % len(devices), i) for i in devices]
    return lax.ppermute(block, axis, route)


def per_device(amplitudes, bra_factor, ket_factor, pair_list):
    tau_rows = lax.all_gather(amplitudes, "occ", axis=2, tiled=True)
    ket_rows = lax.all_gather(ket_factor, "va", axis=0, tiled=True)
    group = bra_factor.shape[0]
    pairs = amplitudes.shape[0]
    cycle_size = lax.axis_size("vb")
    position = lax.axis_index("vb")
    total = jnp.zeros((pairs, bra_factor.shape[2], ket_factor.shape[1]), jnp.float32)
    travelling = bra_factor
    for step in range(cycle_size):
        if step > 0:
            travelling = from_behind(travelling, "vb", 1)
        which = (position - step) % cycle_size
        picks = lax.dynamic_index_in_dim(pair_list, which, 0, keepdims=False)
        chosen = jnp.take(tau_rows, picks, axis=0)
        ket_group = lax.dynamic_slice_in_dim(ket_rows, which * group, group, 0)
        half = jnp.einsum(
            "qbd,kcd->qkcb", ket_group, chosen, preferred_element_type=jnp.float32
        ).astype(jnp.bfloat16)
        partial_terms = jnp.einsum(
            "qca,qkcb->kab", travelling, half, preferred_element_type=jnp.float32
        )
        total = total.at[picks].add(partial_terms)
    return lax.psum_scatter(total, "va", scatter_dimension=1, tiled=True)


def ladder_kernel(
    n, chunks, list_ref, tau_in, bra_in, ket_in, out_ref,
    tau, bra, ket, half, part, outgoing, from_left, from_right,
    local_sem, own_send, own_recv, relay_send, relay_recv, pass_send, pass_recv,
    bra_send, bra_recv, kr_send, kl_recv, kl_send, kr_recv,
    sum_send, left_recv, right_recv,
):
    z, v, o = lax.axis_index("va"), lax.axis_index("vb"), lax.axis_index("occ")
    pairs, c_rows, width = tau_in.shape
    spins = pairs // chunks
    b_rows = ket_in.shape[1]
    part_b = b_rows // chunks
    groups, picks = list_ref.shape
    group = bra_in.shape[0]
    pieces = chunks * spins
    batch = pairs // spins
    xo = o + 1 - 2 * lax.rem(o, 2)
    yo = lax.rem(o + 2, 4)
    do = 3 - o
    sibling = (z, 1 - v, o)
    x_near, y_near = (z, v, xo), (z, v, yo)
    right, left = (z + 1, v, o), (z - 1, v, o)
    has_right, has_left = z < n - 1, z > 0

    def remote(src, dst, send, recv, device):
        return pltpu.make_async_remote_copy(
            src_ref=src, dst_ref=dst, send_sem=send, recv_sem=recv,
            device_id=device, device_id_type=MESH,
        )

    locals_ = [
        pltpu.make_async_copy(tau_in, tau.at[o], local_sem.at[0]),
        pltpu.make_async_copy(ket_in, ket.at[pl.ds(z, 1)], local_sem.at[1]),
        pltpu.make_async_copy(bra_in, bra.at[v], local_sem.at[2]),
    ]
    for copy in locals_:
        copy.start()

    barrier = pltpu.get_barrier_semaphore()
    for near in (sibling, x_near, y_near):
        pl.semaphore_signal(barrier, inc=1, device_id=near, device_id_type=MESH)

    @pl.when(has_right)
    def _():
        pl.semaphore_signal(barrier, inc=1, device_id=right, device_id_type=MESH)

    @pl.when(has_left)
    def _():
        pl.semaphore_signal(barrier, inc=1, device_id=left, device_id_type=MESH)

    pl.semaphore_wait(
        barrier, 3 + jnp.where(has_right, 1, 0) + jnp.where(has_left, 1, 0)
    )

    rows = c_rows // 2
    mine = pl.ds(pl.multiple_of(v * rows, rows), rows)
    other = pl.ds(pl.multiple_of((1 - v) * rows, rows), rows)

    def own(p, way):
        return remote(
            tau_in.at[p, mine], tau.at[o, p, mine],
            own_send.at[way, p], own_recv.at[way, p], (x_near, y_near)[way],
        )

    def own_arrival(p, way):
        block = tau.at[(xo, yo)[way], p, mine]
        return remote(block, block, own_send.at[way, p], own_recv.at[way, p], (x_near, y_near)[way])

    relay_from = jnp.where(v == 0, xo, yo)
    relay_to = (z, v, jnp.where(v == 0, yo, xo))

    def relay(p):
        block = tau.at[relay_from, p, mine]
        return remote(block, block, relay_send.at[p], relay_recv.at[p], relay_to)

    def relay_arrival(p):
        block = tau.at[do, p, mine]
        return remote(block, block, relay_send.at[p], relay_recv.at[p], relay_to)

    def handed(p, k, which):
        block = tau.at[(xo, yo, do)[k], p, which]
        return remote(block, block, pass_send.at[k, p], pass_recv.at[k, p], sibling)

    ahead = 3

    def comm(p):
        own_arrival(p, 0).wait_recv()
        own_arrival(p, 1).wait_recv()
        relay(p).start()
        handed(p, 0, mine).start()
        handed(p, 1, mine).start()
        if p + ahead < pairs:
            own(p + ahead, 0).start()
            own(p + ahead, 1).start()

    def comm_far(p):
        relay_arrival(p).wait_recv()
        handed(p, 2, mine).start()

    def chunk(q, h):
        return ket.at[q, pl.ds(h * part_b, part_b)]

    def to_right(h, hop):
        if hop == 0:
            src = ket_in.at[0, pl.ds(h * part_b, part_b)]
        else:
            src = chunk(z - hop, h)
        return remote(src, chunk(z - hop, h), kr_send.at[hop, h], kl_recv.at[hop, h], right)

    def to_left(h, hop):
        if hop == 0:
            src = ket_in.at[0, pl.ds(h * part_b, part_b)]
        else:
            src = chunk(z + hop, h)
        return remote(src, chunk(z + hop, h), kl_send.at[hop, h], kr_recv.at[hop, h], left)

    def comm_ket(h, hop):
        if hop > 0:
            @pl.when(z - hop >= 0)
            def _():
                block = chunk(z - hop, h)
                remote(block, block, kr_send.at[hop - 1, h], kl_recv.at[hop - 1, h], left).wait_recv()

            @pl.when(z + hop <= n - 1)
            def _():
                block = chunk(z + hop, h)
                remote(block, block, kl_send.at[hop - 1, h], kr_recv.at[hop - 1, h], right).wait_recv()
        if hop < n - 1:
            @pl.when((z - hop >= 0) & has_right)
            def _():
                to_right(h, hop).start()

            @pl.when((z + hop <= n - 1) & has_left)
            def _():
                to_left(h, hop).start()

    def weight(g, p):
        total = jnp.float32(0.0)
        for k in range(picks):
            total = total + jnp.where(list_ref[g, k] == p, 1.0, 0.0)
        return total

    def sum_right(i, t):
        return remote(outgoing.at[i, t], from_left.at[i, t], sum_send.at[i, t], left_recv.at[i, t], right)

    def sum_left(i, t):
        return remote(outgoing.at[i, t], from_right.at[i, t], sum_send.at[i, t], right_recv.at[i, t], left)

    def left_arrival(i, t):
        block = from_left.at[i, t]
        return remote(block, block, sum_send.at[i, t], left_recv.at[i, t], left)

    def right_arrival(i, t):
        block = from_right.at[i, t]
        return remote(block, block, sum_send.at[i, t], right_recv.at[i, t], right)

    order = []
    for k in range((n + 1) // 2):
        order += [n - 1 - k] + ([k] if k != n - 1 - k else [])
    a_rows = bra.shape[3] // n

    def compute(i):
        h, turn = i // spins, lax.rem(i, spins)
        rows_h = pl.ds(pl.multiple_of(h * part_b, part_b), part_b)
        for s in range(batch):
            p = turn * batch + s
            total = None
            for j in range(4):
                lhs = ket[:, rows_h, pl.ds(j * width, width)].reshape(n * part_b, width)
                term = lax.dot_general(lhs, tau[j, p], NT, preferred_element_type=jnp.float32)
                total = term if total is None else total + term
            for q in range(n):
                block = total[q * part_b:(q + 1) * part_b] * weight(q // group, p)
                half[pl.ds(s * part_b, part_b), pl.ds(q * c_rows, c_rows)] = block.astype(jnp.bfloat16)
        for t in order:
            cols = pl.ds(t * a_rows, a_rows)
            right_side = bra[:, :, :, cols].reshape(n * c_rows, a_rows)
            block = jnp.dot(half[...], right_side, preferred_element_type=jnp.float32)
            part[i, t] = block
            if t > 0:
                @pl.when(z == 0)
                def _():
                    outgoing[i, t] = block.astype(jnp.bfloat16)
                    sum_right(i, t).start()
            if t < n - 1:
                @pl.when(z == n - 1)
                def _():
                    outgoing[i, t] = block.astype(jnp.bfloat16)
                    sum_left(i, t).start()

    def combine(i):
        for t in order:
            if t > 1:
                @pl.when((z > 0) & (z < t))
                def _():
                    left_arrival(i, t).wait_recv()
                    outgoing[i, t] = (part[i, t] + from_left[i, t].astype(jnp.float32)).astype(jnp.bfloat16)
                    sum_right(i, t).start()
            if t < n - 2:
                @pl.when((z < n - 1) & (z > t))
                def _():
                    right_arrival(i, t).wait_recv()
                    outgoing[i, t] = (part[i, t] + from_right[i, t].astype(jnp.float32)).astype(jnp.bfloat16)
                    sum_left(i, t).start()

    def finish(i):
        for t in range(n):
            @pl.when(z == t)
            def _():
                if t > 0:
                    left_arrival(i, t).wait_recv()
                    part[i, t] += from_left[i, t].astype(jnp.float32)
                if t < n - 1:
                    right_arrival(i, t).wait_recv()
                    part[i, t] += from_right[i, t].astype(jnp.float32)

    bra_copy = remote(bra_in, bra.at[v], bra_send, bra_recv, sibling)
    for p in range(min(ahead, pairs)):
        own(p, 0).start()
        own(p, 1).start()
    comm_ket(0, 0)
    bra_copy.start()
    for copy in locals_:
        copy.wait()

    def passed(first):
        for s in range(batch):
            for k in range(3):
                handed(first * batch + s, k, other).wait_recv()

    def rest(h):
        for hop in range(2, n):
            yield lambda hop=hop: comm_ket(h, hop)
            if hop == max(2, n - 2) and h + 1 < chunks:
                comm_ket(h + 1, 0)

    def interleave(*streams):
        waiting = [iter(stream) for stream in streams]
        while waiting:
            for stream in list(waiting):
                try:
                    next(stream)()
                except StopIteration:
                    waiting.remove(stream)

    def tau_events(first):
        for s in range(batch):
            p = first * batch + s
            yield lambda p=p: comm(p)
            if s > 0:
                yield lambda p=p: comm_far(p - 1)
        yield lambda: comm_far(first * batch + batch - 1)

    def ket_events(h):
        yield lambda: comm_ket(h, 1)
        yield from rest(h)

    near = tau_events(1)
    interleave(tau_events(0), ket_events(0))
    passed(0)
    remote(bra_in, bra.at[1 - v], bra_send, bra_recv, sibling).wait_recv()
    if chunks > 1:
        comm_ket(1, 1)
    compute(0)
    next(near)()
    if chunks > 1:
        interleave([next(near)], rest(1))
        compute(spins)
    interleave(near, *[ket_events(h) for h in range(2, chunks)])
    combine(0)
    passed(1)
    compute(1)
    if chunks > 1:
        combine(spins)

    def turn(i, carry):
        compute(i)
        combine(jnp.where(i == spins + 1, 1, i - 1))
        return carry

    lax.fori_loop(spins + 1, pieces, turn, 0)

    def close(i, carry):
        finish(i)
        return carry

    combine(pieces - 1)
    lax.fori_loop(0, pieces - 1, close, 0)

    def give(slot):
        for s in range(batch):
            full = jnp.concatenate(
                [part[h * spins + slot, z, pl.ds(s * part_b, part_b), :] for h in range(chunks)], axis=0
            )
            out_ref[slot * batch + s] = full.T

    for slot in range(spins - 1):
        give(slot)
    finish(pieces - 1)
    give(spins - 1)

    for p in range(pairs):
        own(p, 0).wait_send()
        own(p, 1).wait_send()
        relay(p).wait_send()
        for k in range(3):
            handed(p, k, mine).wait_send()
    bra_copy.wait_send()
    for h in range(chunks):
        for hop in range(n - 1):
            @pl.when((z - hop >= 0) & has_right)
            def _():
                to_right(h, hop).wait_send()

            @pl.when((z + hop <= n - 1) & has_left)
            def _():
                to_left(h, hop).wait_send()

    def drain(i, carry):
        for t in range(n):
            @pl.when(z < t)
            def _():
                sum_right(i, t).wait_send()

            @pl.when(z > t)
            def _():
                sum_left(i, t).wait_send()
        return carry

    lax.fori_loop(0, pieces, drain, 0)


def fused_device(n, chunks, amplitudes, bra_factor, ket_factor, pair_list):
    pairs, c_rows, width = amplitudes.shape
    b_rows, depth = ket_factor.shape[1:]
    group, _, columns = bra_factor.shape
    pieces = pairs
    tall = pairs // (pairs // chunks) * (b_rows // chunks)
    a_rows = columns // n
    dma = pltpu.SemaphoreType.DMA
    hbm = pl.BlockSpec(memory_space=pl.ANY)
    return pl.pallas_call(
        functools.partial(ladder_kernel, n, chunks),
        out_shape=jax.ShapeDtypeStruct((pairs, a_rows, b_rows), jnp.float32),
        in_specs=[pl.BlockSpec(memory_space=pltpu.SMEM), hbm, hbm, hbm],
        out_specs=pl.BlockSpec(memory_space=pltpu.VMEM),
        scratch_shapes=[
            pltpu.VMEM((4, pairs, c_rows, width), jnp.bfloat16),
            pltpu.VMEM((2, group, c_rows, columns), jnp.bfloat16),
            pltpu.VMEM((n, b_rows, depth), jnp.bfloat16),
            pltpu.VMEM((tall, n * c_rows), jnp.bfloat16),
            pltpu.VMEM((pieces, n, tall, a_rows), jnp.float32),
            pltpu.VMEM((pieces, n, tall, a_rows), jnp.bfloat16),
            pltpu.VMEM((pieces, n, tall, a_rows), jnp.bfloat16),
            pltpu.VMEM((pieces, n, tall, a_rows), jnp.bfloat16),
            dma((3,)),
            dma((2, pairs)), dma((2, pairs)),
            dma((pairs,)), dma((pairs,)),
            dma((3, pairs)), dma((3, pairs)),
            dma, dma,
            dma((n, chunks)), dma((n, chunks)), dma((n, chunks)), dma((n, chunks)),
            dma((pieces, n)), dma((pieces, n)), dma((pieces, n)),
        ],
        compiler_params=pltpu.CompilerParams(
            collective_id=0, has_side_effects=True, vmem_limit_bytes=60 * 2**20
        ),
    )(pair_list, amplitudes, bra_factor, ket_factor)


def solution(mesh):
    placed = (P(None, "va", "occ"), P("vb", "va", None), P("va", ("vb", "occ"), None), P())
    n = mesh.shape["va"]
    small = mesh.shape["vb"] == 2 and mesh.shape["occ"] == 4

    def body(amplitudes, bra_factor, ket_factor, pair_list):
        chunks = 3
        fits = (
            small
            and amplitudes.shape[0] == 2 * chunks
            and ket_factor.shape[0] == 1
            and 2 * bra_factor.shape[0] == n
            and ket_factor.shape[1] % (16 * chunks) == 0
        )
        if fits:
            return fused_device(n, chunks, amplitudes, bra_factor, ket_factor, pair_list)
        return per_device(amplitudes, bra_factor, ket_factor, pair_list)

    return jax.shard_map(
        body,
        mesh=mesh,
        in_specs=placed,
        out_specs=P(None, "va", ("vb", "occ")),
        check_vma=False,
    )
```

```python
import functools

import jax
import jax.numpy as jnp
from jax import lax
from jax.experimental import pallas as pl
from jax.experimental.pallas import tpu as pltpu
from jax.sharding import PartitionSpec as P

MESH = pl.DeviceIdType.MESH
NT = (((1,), (1,)), ((), ()))


def from_behind(block, axis, distance):
    devices = range(lax.axis_size(axis))
    route = [((i - distance) % len(devices), i) for i in devices]
    return lax.ppermute(block, axis, route)


def per_device(amplitudes, bra_factor, ket_factor, pair_list):
    tau_rows = lax.all_gather(amplitudes, "occ", axis=2, tiled=True)
    ket_rows = lax.all_gather(ket_factor, "va", axis=0, tiled=True)
    group = bra_factor.shape[0]
    pairs = amplitudes.shape[0]
    cycle_size = lax.axis_size("vb")
    position = lax.axis_index("vb")
    total = jnp.zeros((pairs, bra_factor.shape[2], ket_factor.shape[1]), jnp.float32)
    travelling = bra_factor
    for step in range(cycle_size):
        if step > 0:
            travelling = from_behind(travelling, "vb", 1)
        which = (position - step) % cycle_size
        picks = lax.dynamic_index_in_dim(pair_list, which, 0, keepdims=False)
        chosen = jnp.take(tau_rows, picks, axis=0)
        ket_group = lax.dynamic_slice_in_dim(ket_rows, which * group, group, 0)
        half = jnp.einsum(
            "qbd,kcd->qkcb", ket_group, chosen, preferred_element_type=jnp.float32
        ).astype(jnp.bfloat16)
        partial_terms = jnp.einsum(
            "qca,qkcb->kab", travelling, half, preferred_element_type=jnp.float32
        )
        total = total.at[picks].add(partial_terms)
    return lax.psum_scatter(total, "va", scatter_dimension=1, tiled=True)


def ladder_kernel(
    n, chunks, list_ref, tau_in, bra_in, ket_in, out_ref,
    tau, bra, ket, half, part, outgoing, from_left, from_right,
    local_sem, own_send, own_recv, relay_send, relay_recv, pass_send, pass_recv,
    bra_send, bra_recv, kr_send, kl_recv, kl_send, kr_recv,
    sum_send, left_recv, right_recv,
):
    z, v, o = lax.axis_index("va"), lax.axis_index("vb"), lax.axis_index("occ")
    pairs, c_rows, width = tau_in.shape
    spins = pairs // chunks
    b_rows = ket_in.shape[1]
    part_b = b_rows // chunks
    groups, picks = list_ref.shape
    group = bra_in.shape[0]
    pieces = chunks * spins
    batch = pairs // spins
    xo = o + 1 - 2 * lax.rem(o, 2)
    yo = lax.rem(o + 2, 4)
    do = 3 - o
    sibling = (z, 1 - v, o)
    x_near, y_near = (z, v, xo), (z, v, yo)
    right, left = (z + 1, v, o), (z - 1, v, o)
    has_right, has_left = z < n - 1, z > 0

    def remote(src, dst, send, recv, device):
        return pltpu.make_async_remote_copy(
            src_ref=src, dst_ref=dst, send_sem=send, recv_sem=recv,
            device_id=device, device_id_type=MESH,
        )

    locals_ = [
        pltpu.make_async_copy(tau_in, tau.at[o], local_sem.at[0]),
        pltpu.make_async_copy(ket_in, ket.at[pl.ds(z, 1)], local_sem.at[1]),
        pltpu.make_async_copy(bra_in, bra.at[v], local_sem.at[2]),
    ]
    for copy in locals_:
        copy.start()

    barrier = pltpu.get_barrier_semaphore()
    for near in (sibling, x_near, y_near):
        pl.semaphore_signal(barrier, inc=1, device_id=near, device_id_type=MESH)

    @pl.when(has_right)
    def _():
        pl.semaphore_signal(barrier, inc=1, device_id=right, device_id_type=MESH)

    @pl.when(has_left)
    def _():
        pl.semaphore_signal(barrier, inc=1, device_id=left, device_id_type=MESH)

    pl.semaphore_wait(
        barrier, 3 + jnp.where(has_right, 1, 0) + jnp.where(has_left, 1, 0)
    )

    rows = c_rows // 2
    mine = pl.ds(pl.multiple_of(v * rows, rows), rows)
    other = pl.ds(pl.multiple_of((1 - v) * rows, rows), rows)

    def own(p, way):
        return remote(
            tau_in.at[p, mine], tau.at[o, p, mine],
            own_send.at[way, p], own_recv.at[way, p], (x_near, y_near)[way],
        )

    def own_arrival(p, way):
        block = tau.at[(xo, yo)[way], p, mine]
        return remote(block, block, own_send.at[way, p], own_recv.at[way, p], (x_near, y_near)[way])

    relay_from = jnp.where(v == 0, xo, yo)
    relay_to = (z, v, jnp.where(v == 0, yo, xo))

    def relay(p):
        block = tau.at[relay_from, p, mine]
        return remote(block, block, relay_send.at[p], relay_recv.at[p], relay_to)

    def relay_arrival(p):
        block = tau.at[do, p, mine]
        return remote(block, block, relay_send.at[p], relay_recv.at[p], relay_to)

    def handed(p, k, which):
        block = tau.at[(xo, yo, do)[k], p, which]
        return remote(block, block, pass_send.at[k, p], pass_recv.at[k, p], sibling)

    ahead = pairs

    def comm(p):
        own_arrival(p, 0).wait_recv()
        own_arrival(p, 1).wait_recv()
        relay(p).start()
        handed(p, 0, mine).start()
        handed(p, 1, mine).start()
        if p + ahead < pairs:
            own(p + ahead, 0).start()
            own(p + ahead, 1).start()

    def comm_far(p):
        relay_arrival(p).wait_recv()
        handed(p, 2, mine).start()

    def chunk(q, h):
        return ket.at[q, pl.ds(h * part_b, part_b)]

    def to_right(h, hop):
        if hop == 0:
            src = ket_in.at[0, pl.ds(h * part_b, part_b)]
        else:
            src = chunk(z - hop, h)
        return remote(src, chunk(z - hop, h), kr_send.at[hop, h], kl_recv.at[hop, h], right)

    def to_left(h, hop):
        if hop == 0:
            src = ket_in.at[0, pl.ds(h * part_b, part_b)]
        else:
            src = chunk(z + hop, h)
        return remote(src, chunk(z + hop, h), kl_send.at[hop, h], kr_recv.at[hop, h], left)

    def comm_ket(h, hop):
        if hop > 0:
            @pl.when(z - hop >= 0)
            def _():
                block = chunk(z - hop, h)
                remote(block, block, kr_send.at[hop - 1, h], kl_recv.at[hop - 1, h], left).wait_recv()

            @pl.when(z + hop <= n - 1)
            def _():
                block = chunk(z + hop, h)
                remote(block, block, kl_send.at[hop - 1, h], kr_recv.at[hop - 1, h], right).wait_recv()
        if hop < n - 1:
            @pl.when((z - hop >= 0) & has_right)
            def _():
                to_right(h, hop).start()

            @pl.when((z + hop <= n - 1) & has_left)
            def _():
                to_left(h, hop).start()

    def weight(g, p):
        total = jnp.float32(0.0)
        for k in range(picks):
            total = total + jnp.where(list_ref[g, k] == p, 1.0, 0.0)
        return total

    def sum_right(i, t):
        return remote(outgoing.at[i, t], from_left.at[i, t], sum_send.at[i, t], left_recv.at[i, t], right)

    def sum_left(i, t):
        return remote(outgoing.at[i, t], from_right.at[i, t], sum_send.at[i, t], right_recv.at[i, t], left)

    def left_arrival(i, t):
        block = from_left.at[i, t]
        return remote(block, block, sum_send.at[i, t], left_recv.at[i, t], left)

    def right_arrival(i, t):
        block = from_right.at[i, t]
        return remote(block, block, sum_send.at[i, t], right_recv.at[i, t], right)

    order = []
    for k in range((n + 1) // 2):
        order += [n - 1 - k] + ([k] if k != n - 1 - k else [])
    a_rows = bra.shape[3] // n

    def compute(i):
        h, turn = i // spins, lax.rem(i, spins)
        rows_h = pl.ds(pl.multiple_of(h * part_b, part_b), part_b)
        for s in range(batch):
            p = turn * batch + s
            total = None
            for j in range(4):
                lhs = ket[:, rows_h, pl.ds(j * width, width)].reshape(n * part_b, width)
                term = lax.dot_general(lhs, tau[j, p], NT, preferred_element_type=jnp.float32)
                total = term if total is None else total + term
            for q in range(n):
                block = total[q * part_b:(q + 1) * part_b] * weight(q // group, p)
                half[pl.ds(s * part_b, part_b), pl.ds(q * c_rows, c_rows)] = block.astype(jnp.bfloat16)
        for t in order:
            cols = pl.ds(t * a_rows, a_rows)
            right_side = bra[:, :, :, cols].reshape(n * c_rows, a_rows)
            block = jnp.dot(half[...], right_side, preferred_element_type=jnp.float32)
            part[i, t] = block
            if t > 0:
                @pl.when(z == 0)
                def _():
                    outgoing[i, t] = block.astype(jnp.bfloat16)
                    sum_right(i, t).start()
            if t < n - 1:
                @pl.when(z == n - 1)
                def _():
                    outgoing[i, t] = block.astype(jnp.bfloat16)
                    sum_left(i, t).start()

    def combine(i):
        for t in order:
            if t > 1:
                @pl.when((z > 0) & (z < t))
                def _():
                    left_arrival(i, t).wait_recv()
                    outgoing[i, t] = (part[i, t] + from_left[i, t].astype(jnp.float32)).astype(jnp.bfloat16)
                    sum_right(i, t).start()
            if t < n - 2:
                @pl.when((z < n - 1) & (z > t))
                def _():
                    right_arrival(i, t).wait_recv()
                    outgoing[i, t] = (part[i, t] + from_right[i, t].astype(jnp.float32)).astype(jnp.bfloat16)
                    sum_left(i, t).start()

    def finish(i):
        for t in range(n):
            @pl.when(z == t)
            def _():
                if t > 0:
                    left_arrival(i, t).wait_recv()
                    part[i, t] += from_left[i, t].astype(jnp.float32)
                if t < n - 1:
                    right_arrival(i, t).wait_recv()
                    part[i, t] += from_right[i, t].astype(jnp.float32)

    bra_copy = remote(bra_in, bra.at[v], bra_send, bra_recv, sibling)
    for p in range(min(ahead, pairs)):
        own(p, 0).start()
        own(p, 1).start()
    comm_ket(0, 0)
    comm_ket(1, 0)
    bra_copy.start()
    for copy in locals_:
        copy.wait()

    def passed(first):
        for s in range(batch):
            for k in range(3):
                handed(first * batch + s, k, other).wait_recv()

    at_end = (z == 0) | (z == n - 1)

    def early(first, last):
        for p in range(first, last):
            comm(p)

    def late(h):
        for hop in range(2, n - 1):
            comm_ket(h, hop)

    def own_chunk(h):
        if h < chunks:
            comm_ket(h, 0)

    third = batch
    comm(0)
    comm_ket(0, 1)
    early(1, third - 1)
    comm_ket(1, 1)
    early(third - 1, third + 1)
    late(0)
    own_chunk(2)
    early(third + 1, pairs)
    for h in range(2, chunks):
        comm_ket(h, 1)
    comm_far(0)
    late(1)
    for p in range(1, batch):
        comm_far(p)
    passed(0)
    remote(bra_in, bra.at[1 - v], bra_send, bra_recv, sibling).wait_recv()
    comm_ket(0, n - 1)

    @pl.when(at_end)
    def _():
        compute(0)

    for h in range(2, chunks):
        late(h)
    for p in range(batch, pairs):
        comm_far(p)
    for first in range(1, spins):
        passed(first)

    def middle(i, carry):
        compute(i)
        return carry

    lax.fori_loop(jnp.where(at_end, 1, 0), 2, middle, 0)
    for h in range(1, chunks):
        comm_ket(h, n - 1)
    combine(0)

    def turn(i, carry):
        compute(i)
        combine(i - 1)
        return carry

    lax.fori_loop(2, pieces, turn, 0)

    def close(i, carry):
        finish(i)
        return carry

    combine(pieces - 1)
    lax.fori_loop(0, pieces - 1, close, 0)

    def give(slot):
        for s in range(batch):
            full = jnp.concatenate(
                [part[h * spins + slot, z, pl.ds(s * part_b, part_b), :] for h in range(chunks)], axis=0
            )
            out_ref[slot * batch + s] = full.T

    for slot in range(spins - 1):
        give(slot)
    finish(pieces - 1)
    give(spins - 1)

    for p in range(pairs):
        own(p, 0).wait_send()
        own(p, 1).wait_send()
        relay(p).wait_send()
        for k in range(3):
            handed(p, k, mine).wait_send()
    bra_copy.wait_send()
    for h in range(chunks):
        for hop in range(n - 1):
            @pl.when((z - hop >= 0) & has_right)
            def _():
                to_right(h, hop).wait_send()

            @pl.when((z + hop <= n - 1) & has_left)
            def _():
                to_left(h, hop).wait_send()

    def drain(i, carry):
        for t in range(n):
            @pl.when(z < t)
            def _():
                sum_right(i, t).wait_send()

            @pl.when(z > t)
            def _():
                sum_left(i, t).wait_send()
        return carry

    lax.fori_loop(0, pieces, drain, 0)


def fused_device(n, chunks, amplitudes, bra_factor, ket_factor, pair_list):
    pairs, c_rows, width = amplitudes.shape
    b_rows, depth = ket_factor.shape[1:]
    group, _, columns = bra_factor.shape
    pieces = pairs
    tall = pairs // (pairs // chunks) * (b_rows // chunks)
    a_rows = columns // n
    dma = pltpu.SemaphoreType.DMA
    hbm = pl.BlockSpec(memory_space=pl.ANY)
    return pl.pallas_call(
        functools.partial(ladder_kernel, n, chunks),
        out_shape=jax.ShapeDtypeStruct((pairs, a_rows, b_rows), jnp.float32),
        in_specs=[pl.BlockSpec(memory_space=pltpu.SMEM), hbm, hbm, hbm],
        out_specs=pl.BlockSpec(memory_space=pltpu.VMEM),
        scratch_shapes=[
            pltpu.VMEM((4, pairs, c_rows, width), jnp.bfloat16),
            pltpu.VMEM((2, group, c_rows, columns), jnp.bfloat16),
            pltpu.VMEM((n, b_rows, depth), jnp.bfloat16),
            pltpu.VMEM((tall, n * c_rows), jnp.bfloat16),
            pltpu.VMEM((pieces, n, tall, a_rows), jnp.float32),
            pltpu.VMEM((pieces, n, tall, a_rows), jnp.bfloat16),
            pltpu.VMEM((pieces, n, tall, a_rows), jnp.bfloat16),
            pltpu.VMEM((pieces, n, tall, a_rows), jnp.bfloat16),
            dma((3,)),
            dma((2, pairs)), dma((2, pairs)),
            dma((pairs,)), dma((pairs,)),
            dma((3, pairs)), dma((3, pairs)),
            dma, dma,
            dma((n, chunks)), dma((n, chunks)), dma((n, chunks)), dma((n, chunks)),
            dma((pieces, n)), dma((pieces, n)), dma((pieces, n)),
        ],
        compiler_params=pltpu.CompilerParams(
            collective_id=0, has_side_effects=True, vmem_limit_bytes=60 * 2**20
        ),
    )(pair_list, amplitudes, bra_factor, ket_factor)


def solution(mesh):
    placed = (P(None, "va", "occ"), P("vb", "va", None), P("va", ("vb", "occ"), None), P())
    n = mesh.shape["va"]
    small = mesh.shape["vb"] == 2 and mesh.shape["occ"] == 4

    def body(amplitudes, bra_factor, ket_factor, pair_list):
        chunks = 3
        fits = (
            small
            and n > 2
            and amplitudes.shape[0] == 2 * chunks
            and ket_factor.shape[0] == 1
            and 2 * bra_factor.shape[0] == n
            and ket_factor.shape[1] % (16 * chunks) == 0
        )
        if fits:
            return fused_device(n, chunks, amplitudes, bra_factor, ket_factor, pair_list)
        return per_device(amplitudes, bra_factor, ket_factor, pair_list)

    return jax.shard_map(
        body,
        mesh=mesh,
        in_specs=placed,
        out_specs=P(None, "va", ("vb", "occ")),
        check_vma=False,
    )
```

```python
import functools

import jax
import jax.numpy as jnp
from jax import lax
from jax.experimental import pallas as pl
from jax.experimental.pallas import tpu as pltpu
from jax.sharding import PartitionSpec as P

MESH = pl.DeviceIdType.MESH
NT = (((1,), (1,)), ((), ()))


def from_behind(block, axis, distance):
    devices = range(lax.axis_size(axis))
    route = [((i - distance) % len(devices), i) for i in devices]
    return lax.ppermute(block, axis, route)


def per_device(amplitudes, bra_factor, ket_factor, pair_list):
    tau_rows = lax.all_gather(amplitudes, "occ", axis=2, tiled=True)
    ket_rows = lax.all_gather(ket_factor, "va", axis=0, tiled=True)
    group = bra_factor.shape[0]
    pairs = amplitudes.shape[0]
    cycle_size = lax.axis_size("vb")
    position = lax.axis_index("vb")
    total = jnp.zeros((pairs, bra_factor.shape[2], ket_factor.shape[1]), jnp.float32)
    travelling = bra_factor
    for step in range(cycle_size):
        if step > 0:
            travelling = from_behind(travelling, "vb", 1)
        which = (position - step) % cycle_size
        picks = lax.dynamic_index_in_dim(pair_list, which, 0, keepdims=False)
        chosen = jnp.take(tau_rows, picks, axis=0)
        ket_group = lax.dynamic_slice_in_dim(ket_rows, which * group, group, 0)
        half = jnp.einsum(
            "qbd,kcd->qkcb", ket_group, chosen, preferred_element_type=jnp.float32
        ).astype(jnp.bfloat16)
        partial_terms = jnp.einsum(
            "qca,qkcb->kab", travelling, half, preferred_element_type=jnp.float32
        )
        total = total.at[picks].add(partial_terms)
    return lax.psum_scatter(total, "va", scatter_dimension=1, tiled=True)


def ladder_kernel(
    n, chunks, list_ref, tau_in, bra_in, ket_in, out_ref,
    tau, bra, ket, half, part, outgoing, from_left, from_right,
    local_sem, own_send, own_recv, relay_send, relay_recv, pass_send, pass_recv,
    bra_send, bra_recv, kr_send, kl_recv, kl_send, kr_recv,
    sum_send, left_recv, right_recv,
):
    z, v, o = lax.axis_index("va"), lax.axis_index("vb"), lax.axis_index("occ")
    pairs, c_rows, width = tau_in.shape
    spins = pairs // chunks
    b_rows = ket_in.shape[1]
    part_b = b_rows // chunks
    groups, picks = list_ref.shape
    group = bra_in.shape[0]
    pieces = chunks * spins
    batch = pairs // spins
    xo = o + 1 - 2 * lax.rem(o, 2)
    yo = lax.rem(o + 2, 4)
    do = 3 - o
    sibling = (z, 1 - v, o)
    x_near, y_near = (z, v, xo), (z, v, yo)
    right, left = (z + 1, v, o), (z - 1, v, o)
    has_right, has_left = z < n - 1, z > 0

    def remote(src, dst, send, recv, device):
        return pltpu.make_async_remote_copy(
            src_ref=src, dst_ref=dst, send_sem=send, recv_sem=recv,
            device_id=device, device_id_type=MESH,
        )

    locals_ = [
        pltpu.make_async_copy(tau_in, tau.at[o], local_sem.at[0]),
        pltpu.make_async_copy(ket_in, ket.at[pl.ds(z, 1)], local_sem.at[1]),
        pltpu.make_async_copy(bra_in, bra.at[v], local_sem.at[2]),
    ]
    for copy in locals_:
        copy.start()

    barrier = pltpu.get_barrier_semaphore()
    for near in (sibling, x_near, y_near):
        pl.semaphore_signal(barrier, inc=1, device_id=near, device_id_type=MESH)

    @pl.when(has_right)
    def _():
        pl.semaphore_signal(barrier, inc=1, device_id=right, device_id_type=MESH)

    @pl.when(has_left)
    def _():
        pl.semaphore_signal(barrier, inc=1, device_id=left, device_id_type=MESH)

    pl.semaphore_wait(
        barrier, 3 + jnp.where(has_right, 1, 0) + jnp.where(has_left, 1, 0)
    )

    rows = c_rows // 2
    mine = pl.ds(pl.multiple_of(v * rows, rows), rows)
    other = pl.ds(pl.multiple_of((1 - v) * rows, rows), rows)

    def own(p, way):
        return remote(
            tau_in.at[p, mine], tau.at[o, p, mine],
            own_send.at[way, p], own_recv.at[way, p], (x_near, y_near)[way],
        )

    def own_arrival(p, way):
        block = tau.at[(xo, yo)[way], p, mine]
        return remote(block, block, own_send.at[way, p], own_recv.at[way, p], (x_near, y_near)[way])

    relay_from = jnp.where(v == 0, xo, yo)
    relay_to = (z, v, jnp.where(v == 0, yo, xo))

    def relay(p):
        block = tau.at[relay_from, p, mine]
        return remote(block, block, relay_send.at[p], relay_recv.at[p], relay_to)

    def relay_arrival(p):
        block = tau.at[do, p, mine]
        return remote(block, block, relay_send.at[p], relay_recv.at[p], relay_to)

    def handed(p, k, which):
        block = tau.at[(xo, yo, do)[k], p, which]
        return remote(block, block, pass_send.at[k, p], pass_recv.at[k, p], sibling)

    ahead = pairs

    def comm(p):
        own_arrival(p, 0).wait_recv()
        own_arrival(p, 1).wait_recv()
        relay(p).start()
        handed(p, 0, mine).start()
        handed(p, 1, mine).start()
        if p + ahead < pairs:
            own(p + ahead, 0).start()
            own(p + ahead, 1).start()

    def comm_far(p):
        relay_arrival(p).wait_recv()
        handed(p, 2, mine).start()

    def chunk(q, h):
        return ket.at[q, pl.ds(h * part_b, part_b)]

    def to_right(h, hop):
        if hop == 0:
            src = ket_in.at[0, pl.ds(h * part_b, part_b)]
        else:
            src = chunk(z - hop, h)
        return remote(src, chunk(z - hop, h), kr_send.at[hop, h], kl_recv.at[hop, h], right)

    def to_left(h, hop):
        if hop == 0:
            src = ket_in.at[0, pl.ds(h * part_b, part_b)]
        else:
            src = chunk(z + hop, h)
        return remote(src, chunk(z + hop, h), kl_send.at[hop, h], kr_recv.at[hop, h], left)

    def comm_ket(h, hop):
        if hop > 0:
            @pl.when(z - hop >= 0)
            def _():
                block = chunk(z - hop, h)
                remote(block, block, kr_send.at[hop - 1, h], kl_recv.at[hop - 1, h], left).wait_recv()

            @pl.when(z + hop <= n - 1)
            def _():
                block = chunk(z + hop, h)
                remote(block, block, kl_send.at[hop - 1, h], kr_recv.at[hop - 1, h], right).wait_recv()
        if hop < n - 1:
            @pl.when((z - hop >= 0) & has_right)
            def _():
                to_right(h, hop).start()

            @pl.when((z + hop <= n - 1) & has_left)
            def _():
                to_left(h, hop).start()

    def weight(g, p):
        total = jnp.float32(0.0)
        for k in range(picks):
            total = total + jnp.where(list_ref[g, k] == p, 1.0, 0.0)
        return total

    def sum_right(i, t):
        return remote(outgoing.at[i, t], from_left.at[i, t], sum_send.at[i, t], left_recv.at[i, t], right)

    def sum_left(i, t):
        return remote(outgoing.at[i, t], from_right.at[i, t], sum_send.at[i, t], right_recv.at[i, t], left)

    def left_arrival(i, t):
        block = from_left.at[i, t]
        return remote(block, block, sum_send.at[i, t], left_recv.at[i, t], left)

    def right_arrival(i, t):
        block = from_right.at[i, t]
        return remote(block, block, sum_send.at[i, t], right_recv.at[i, t], right)

    order = []
    for k in range((n + 1) // 2):
        order += [n - 1 - k] + ([k] if k != n - 1 - k else [])
    a_rows = bra.shape[3] // n

    def compute(i):
        h, turn = i // spins, lax.rem(i, spins)
        rows_h = pl.ds(pl.multiple_of(h * part_b, part_b), part_b)
        for s in range(batch):
            p = turn * batch + s
            total = None
            for j in range(4):
                lhs = ket[:, rows_h, pl.ds(j * width, width)].reshape(n * part_b, width)
                term = lax.dot_general(lhs, tau[j, p], NT, preferred_element_type=jnp.float32)
                total = term if total is None else total + term
            for q in range(n):
                block = total[q * part_b:(q + 1) * part_b] * weight(q // group, p)
                half[pl.ds(s * part_b, part_b), pl.ds(q * c_rows, c_rows)] = block.astype(jnp.bfloat16)
        for t in order:
            cols = pl.ds(t * a_rows, a_rows)
            right_side = bra[:, :, :, cols].reshape(n * c_rows, a_rows)
            block = jnp.dot(half[...], right_side, preferred_element_type=jnp.float32)
            part[i, t] = block
            if t > 0:
                @pl.when(z == 0)
                def _():
                    outgoing[i, t] = block.astype(jnp.bfloat16)
                    sum_right(i, t).start()
            if t < n - 1:
                @pl.when(z == n - 1)
                def _():
                    outgoing[i, t] = block.astype(jnp.bfloat16)
                    sum_left(i, t).start()

    def combine(i):
        for t in order:
            if t > 1:
                @pl.when((z > 0) & (z < t))
                def _():
                    left_arrival(i, t).wait_recv()
                    outgoing[i, t] = (part[i, t] + from_left[i, t].astype(jnp.float32)).astype(jnp.bfloat16)
                    sum_right(i, t).start()
            if t < n - 2:
                @pl.when((z < n - 1) & (z > t))
                def _():
                    right_arrival(i, t).wait_recv()
                    outgoing[i, t] = (part[i, t] + from_right[i, t].astype(jnp.float32)).astype(jnp.bfloat16)
                    sum_left(i, t).start()

    def finish(i):
        for t in range(n):
            @pl.when(z == t)
            def _():
                if t > 0:
                    left_arrival(i, t).wait_recv()
                    part[i, t] += from_left[i, t].astype(jnp.float32)
                if t < n - 1:
                    right_arrival(i, t).wait_recv()
                    part[i, t] += from_right[i, t].astype(jnp.float32)

    bra_copy = remote(bra_in, bra.at[v], bra_send, bra_recv, sibling)
    for h in range(chunks):
        comm_ket(h, 0)
    bra_copy.start()
    for p in range(min(ahead, pairs)):
        own(p, 0).start()
        own(p, 1).start()
    for copy in locals_:
        copy.wait()

    def passed(first):
        for s in range(batch):
            for k in range(3):
                handed(first * batch + s, k, other).wait_recv()

    at_end = (z == 0) | (z == n - 1)

    def early(first, last):
        for p in range(first, last):
            comm(p)

    def late(h):
        for hop in range(2, n - 1):
            comm_ket(h, hop)

    third = batch
    comm(0)
    comm_ket(0, 1)
    early(1, third - 1)
    comm_ket(1, 1)
    early(third - 1, third + 1)
    late(0)
    early(third + 1, pairs)
    for h in range(2, chunks):
        comm_ket(h, 1)
    comm_far(0)
    late(1)
    for p in range(1, batch):
        comm_far(p)
    passed(0)
    remote(bra_in, bra.at[1 - v], bra_send, bra_recv, sibling).wait_recv()
    comm_ket(0, n - 1)

    @pl.when(at_end)
    def _():
        compute(0)

    for h in range(2, chunks):
        late(h)
    for p in range(batch, pairs):
        comm_far(p)
    for first in range(1, spins):
        passed(first)

    def middle(i, carry):
        compute(i)
        return carry

    lax.fori_loop(jnp.where(at_end, 1, 0), 2, middle, 0)
    for h in range(1, chunks):
        comm_ket(h, n - 1)
    combine(0)

    def turn(i, carry):
        compute(i)
        combine(i - 1)
        return carry

    lax.fori_loop(2, pieces, turn, 0)

    def close(i, carry):
        finish(i)
        return carry

    combine(pieces - 1)
    lax.fori_loop(0, pieces - 1, close, 0)

    def give(slot):
        for s in range(batch):
            full = jnp.concatenate(
                [part[h * spins + slot, z, pl.ds(s * part_b, part_b), :] for h in range(chunks)], axis=0
            )
            out_ref[slot * batch + s] = full.T

    for slot in range(spins - 1):
        give(slot)
    finish(pieces - 1)
    give(spins - 1)

    for p in range(pairs):
        own(p, 0).wait_send()
        own(p, 1).wait_send()
        relay(p).wait_send()
        for k in range(3):
            handed(p, k, mine).wait_send()
    bra_copy.wait_send()
    for h in range(chunks):
        for hop in range(n - 1):
            @pl.when((z - hop >= 0) & has_right)
            def _():
                to_right(h, hop).wait_send()

            @pl.when((z + hop <= n - 1) & has_left)
            def _():
                to_left(h, hop).wait_send()

    def drain(i, carry):
        for t in range(n):
            @pl.when(z < t)
            def _():
                sum_right(i, t).wait_send()

            @pl.when(z > t)
            def _():
                sum_left(i, t).wait_send()
        return carry

    lax.fori_loop(0, pieces, drain, 0)


def fused_device(n, chunks, amplitudes, bra_factor, ket_factor, pair_list):
    pairs, c_rows, width = amplitudes.shape
    b_rows, depth = ket_factor.shape[1:]
    group, _, columns = bra_factor.shape
    pieces = pairs
    tall = pairs // (pairs // chunks) * (b_rows // chunks)
    a_rows = columns // n
    dma = pltpu.SemaphoreType.DMA
    hbm = pl.BlockSpec(memory_space=pl.ANY)
    return pl.pallas_call(
        functools.partial(ladder_kernel, n, chunks),
        out_shape=jax.ShapeDtypeStruct((pairs, a_rows, b_rows), jnp.float32),
        in_specs=[pl.BlockSpec(memory_space=pltpu.SMEM), hbm, hbm, hbm],
        out_specs=pl.BlockSpec(memory_space=pltpu.VMEM),
        scratch_shapes=[
            pltpu.VMEM((4, pairs, c_rows, width), jnp.bfloat16),
            pltpu.VMEM((2, group, c_rows, columns), jnp.bfloat16),
            pltpu.VMEM((n, b_rows, depth), jnp.bfloat16),
            pltpu.VMEM((tall, n * c_rows), jnp.bfloat16),
            pltpu.VMEM((pieces, n, tall, a_rows), jnp.float32),
            pltpu.VMEM((pieces, n, tall, a_rows), jnp.bfloat16),
            pltpu.VMEM((pieces, n, tall, a_rows), jnp.bfloat16),
            pltpu.VMEM((pieces, n, tall, a_rows), jnp.bfloat16),
            dma((3,)),
            dma((2, pairs)), dma((2, pairs)),
            dma((pairs,)), dma((pairs,)),
            dma((3, pairs)), dma((3, pairs)),
            dma, dma,
            dma((n, chunks)), dma((n, chunks)), dma((n, chunks)), dma((n, chunks)),
            dma((pieces, n)), dma((pieces, n)), dma((pieces, n)),
        ],
        compiler_params=pltpu.CompilerParams(
            collective_id=0, has_side_effects=True, vmem_limit_bytes=60 * 2**20
        ),
    )(pair_list, amplitudes, bra_factor, ket_factor)


def solution(mesh):
    placed = (P(None, "va", "occ"), P("vb", "va", None), P("va", ("vb", "occ"), None), P())
    n = mesh.shape["va"]
    small = mesh.shape["vb"] == 2 and mesh.shape["occ"] == 4

    def body(amplitudes, bra_factor, ket_factor, pair_list):
        chunks = 3
        fits = (
            small
            and n > 2
            and amplitudes.shape[0] == 2 * chunks
            and ket_factor.shape[0] == 1
            and 2 * bra_factor.shape[0] == n
            and ket_factor.shape[1] % (16 * chunks) == 0
        )
        if fits:
            return fused_device(n, chunks, amplitudes, bra_factor, ket_factor, pair_list)
        return per_device(amplitudes, bra_factor, ket_factor, pair_list)

    return jax.shard_map(
        body,
        mesh=mesh,
        in_specs=placed,
        out_specs=P(None, "va", ("vb", "occ")),
        check_vma=False,
    )
```
